32 devices in a mesh: seq: 8 (over z, y), head: 4 (over x, core).
Axes of the slice: x: 2, y: 2, z: 4, core: 2. Of those that a mesh axis runs over, the one named last changes fastest.
Arguments:
- q_old: bfloat16 [1792, 2048], P(('seq', 'head')), may hold values from -6 to 6
- k_old: bfloat16 [1792, 1024], P(('seq', 'head')), may hold values from -6 to 6
- value_old_layout: bfloat16 [1792, 1024], P(('seq', 'head')), may hold values from -6 to 6
- dout_old: bfloat16 [1792, 2048], P(('seq', 'head')), may hold values from -6 to 6
- old_offsets: int32 [9], replicated, may hold values from 0 to 1024, as said below
- new_offsets: int32 [9], replicated, may hold values from 0 to 1024, as said below
Outputs:
- attn_out: bfloat16 [1792, 2048], P('seq', 'head')
- grad_query_out: bfloat16 [1792, 2048], P('seq', 'head')
- grad_key_out: bfloat16 [1792, 1024], P('seq', 'head')
- grad_value_out: bfloat16 [1792, 1024], P('seq', 'head')
The draws below stay inside these ranges and needn't reach their ends.
Inputs may be any that keep to these rules, and one draw needn't show every extreme that they name: old_offsets[0] = 0 and old_offsets[8] = 1024; old_offsets[j] lies within 48 of j * 128, at exactly -48 for some j and +48 for some j; some block has exactly 224 positions. new_offsets[0] = 0 and new_offsets[8] = 1024; new_offsets[j] lies within 48 of j * 128, at exactly -48 for some j and +48 for some j; some block has exactly 224 positions; for some j, 96 positions of old block j lie in new block j + 1, and for some j, 96 positions of old block j lie in new block j - 1.
All inputs are finite; a program needn't handle non-finite values.
Results may differ from the reference program's by a relative error of at most 0.02.
Values may be sent and summed in bfloat16 or wider, within the bound.
A program may use at most 64 MiB of HBM per device.

```python
import jax
import jax.numpy as jnp
from jax import lax

TOK_DEV = 128
ATTEND_WINDOW = 1024
QUERY_HEADS = 16
KEY_VALUE_HEADS = 8
HEAD_SIZE = 128
SLACK = 48
BLOCK_SLOTS = 224
SEQUENCE_TOKENS = 1024
LAYOUT_SLOTS = 1792
N_SEQ = 8


def ownership(key):
    boundary = jnp.arange(N_SEQ + 1, dtype=jnp.int32)
    old_shift = jax.random.randint(jax.random.fold_in(key, 101), (N_SEQ + 1,), -SLACK, SLACK + 1, dtype=jnp.int32)
    new_shift = jax.random.randint(jax.random.fold_in(key, 102), (N_SEQ + 1,), -SLACK, SLACK + 1, dtype=jnp.int32)
    outer_ends = (boundary == 0) | (boundary == N_SEQ)
    old_shift = jnp.where(outer_ends, 0, old_shift)
    new_shift = jnp.where(outer_ends, 0, new_shift)
    wide_block = jax.random.randint(jax.random.fold_in(key, 103), (), 1, N_SEQ // 2 - 1, dtype=jnp.int32)
    late_block = jax.random.randint(jax.random.fold_in(key, 104), (), N_SEQ // 2, N_SEQ, dtype=jnp.int32)
    old_shift = jnp.where(boundary == wide_block, -SLACK, old_shift)
    old_shift = jnp.where(boundary == wide_block + 1, SLACK, old_shift)
    new_shift = jnp.where(boundary == wide_block + 1, -SLACK, new_shift)
    new_shift = jnp.where(boundary == wide_block + 2, SLACK, new_shift)
    old_shift = jnp.where(boundary == late_block, -SLACK, old_shift)
    new_shift = jnp.where(boundary == late_block, SLACK, new_shift)
    return ((boundary * TOK_DEV + old_shift).astype(jnp.int32), (boundary * TOK_DEV + new_shift).astype(jnp.int32))


def draw_old_offsets(key, part):
    return ownership(key)[0]


def draw_new_offsets(key, part):
    return ownership(key)[1]


def draw_q_old(key, part):
    scenery_backdrop = jnp.clip(jax.random.normal(jax.random.fold_in(key, 211), (LAYOUT_SLOTS, QUERY_HEADS * HEAD_SIZE)), -6.0, 6.0)
    return scenery_backdrop.astype(jnp.bfloat16)


def draw_k_old(key, part):
    scenery_backdrop = jnp.clip(jax.random.normal(jax.random.fold_in(key, 212), (LAYOUT_SLOTS, KEY_VALUE_HEADS * HEAD_SIZE)), -6.0, 6.0)
    return scenery_backdrop.astype(jnp.bfloat16)


def level_of(own_key, dims, shards, smallest, high):
    factor_of = 1.0
    for position, parts in shards:
        draws = jax.random.uniform(jax.random.fold_in(jax.random.fold_in(own_key, 6), position), (parts,), jnp.float32, smallest / len(shards), high / len(shards))
        factor_of = factor_of * jnp.repeat(jnp.exp(draws), dims[position] // parts).reshape((-1,) + (1,) * (len(dims) - 1 - position))
    return factor_of


def centred(stream_key, shape, deviation, most, split=(), kind=jnp.bfloat16):
    factor_of = level_of(stream_key, shape, split, -0.22, 0.18) if split else 1.0
    entries = jax.random.normal(stream_key, shape, jnp.float32) * deviation * factor_of
    return jnp.minimum(jnp.maximum(entries, -most), most).astype(kind)


def setup_inputs(seed: int = 0) -> dict:
    key_of = jax.random.split(jax.random.key(seed), 7)
    return {
        "q_old": draw_q_old(jax.random.fold_in(key_of[6], 71), 0),
        "k_old": draw_k_old(jax.random.fold_in(key_of[6], 71), 0),
        "value_old_layout": centred(key_of[2], (LAYOUT_SLOTS, KEY_VALUE_HEADS * HEAD_SIZE), 1.0, 6.0, ((0, 32),)),
        "dout_old": centred(key_of[3], (LAYOUT_SLOTS, QUERY_HEADS * HEAD_SIZE), 1.0, 6.0, ((0, 32),)),
        "old_offsets": draw_old_offsets(jax.random.fold_in(key_of[6], 71), 0),
        "new_offsets": draw_new_offsets(jax.random.fold_in(key_of[6], 71), 0),
    }


query_scale = 168.0 ** -0.5


def gather_rows(slot_data, offsets):
    positions = jnp.arange(SEQUENCE_TOKENS, dtype=jnp.int32)
    owners = jnp.sum((positions[:, None] >= offsets[None, 1:N_SEQ]).astype(jnp.int32), axis=1).astype(jnp.int32)
    picked = (owners * BLOCK_SLOTS + positions - offsets[owners]).astype(jnp.int32)
    return jnp.take(slot_data, picked, axis=0)


def place_rows(full_rows, offsets):
    slot_index = jnp.arange(LAYOUT_SLOTS, dtype=jnp.int32)
    owners = (slot_index // BLOCK_SLOTS).astype(jnp.int32)
    positions = (offsets[owners] + slot_index % BLOCK_SLOTS).astype(jnp.int32)
    is_live = positions < offsets[owners + 1]
    picked = jnp.clip(positions, 0, SEQUENCE_TOKENS - 1).astype(jnp.int32)
    return jnp.where(is_live[:, None], jnp.take(full_rows, picked, axis=0), jnp.zeros((), full_rows.dtype))


def attend_block(queries, grads_out, key_rows, value_rows, allowed):
    heads_per_group = QUERY_HEADS // KEY_VALUE_HEADS
    key_full = jnp.repeat(key_rows.astype(jnp.float32), heads_per_group, axis=1)
    value_full = jnp.repeat(value_rows.astype(jnp.float32), heads_per_group, axis=1)
    query_full = queries.astype(jnp.float32)
    grad_full = grads_out.astype(jnp.float32)
    scores = jnp.einsum("rhd,lhd->hrl", query_full, key_full) * query_scale
    scores = jnp.where(allowed[None], scores, -1e30)
    row_max = jnp.max(scores, axis=2, keepdims=True)
    weights = jnp.where(allowed[None], jnp.exp(scores - row_max), 0.0)
    probabilities = weights / jnp.sum(weights, axis=2, keepdims=True)
    rounded = lax.optimization_barrier(probabilities.astype(jnp.bfloat16)).astype(jnp.float32)
    attn = jnp.einsum("hrl,lhd->rhd", rounded, value_full).astype(jnp.bfloat16)
    attn_full = lax.optimization_barrier(attn).astype(jnp.float32)
    row_delta = jnp.transpose(jnp.sum(grad_full * attn_full, axis=2))[:, :, None]
    grad_prob = jnp.einsum("rhd,lhd->hrl", grad_full, value_full)
    grad_score = (probabilities * (grad_prob - row_delta) * query_scale).astype(jnp.bfloat16)
    score_full = lax.optimization_barrier(grad_score).astype(jnp.float32)
    grad_query = jnp.einsum("hrl,lhd->rhd", score_full, key_full).astype(jnp.bfloat16)
    key_extent = key_rows.shape[0]
    key_gradient = jnp.einsum("hrl,rhd->lhd", score_full, query_full)
    value_gradient = jnp.einsum("hrl,rhd->lhd", rounded, grad_full)
    key_gradient = jnp.sum(key_gradient.reshape(key_extent, KEY_VALUE_HEADS, heads_per_group, HEAD_SIZE), axis=2)
    value_gradient = jnp.sum(value_gradient.reshape(key_extent, KEY_VALUE_HEADS, heads_per_group, HEAD_SIZE), axis=2)
    return attn, grad_query, key_gradient, value_gradient


def reference(q_old, k_old, value_old_layout, dout_old, old_offsets, new_offsets):
    queries = gather_rows(q_old, old_offsets)
    key_rows = gather_rows(k_old, old_offsets)
    value_rows = gather_rows(value_old_layout, old_offsets)
    grads_out = gather_rows(dout_old, old_offsets)
    pad_amount_rows = jnp.zeros((ATTEND_WINDOW, KEY_VALUE_HEADS * HEAD_SIZE), jnp.bfloat16)
    padded_keys = jnp.concatenate([pad_amount_rows, key_rows], axis=0)
    padded_values = jnp.concatenate([pad_amount_rows, value_rows], axis=0)
    key_extent = ATTEND_WINDOW + TOK_DEV

    def block_step(running, block_number):
        key_accumulator, value_accumulator = running
        row_begin = (block_number * TOK_DEV).astype(jnp.int32)
        query_block = lax.dynamic_slice_in_dim(queries, row_begin, TOK_DEV, 0).reshape(TOK_DEV, QUERY_HEADS, HEAD_SIZE)
        grad_block = lax.dynamic_slice_in_dim(grads_out, row_begin, TOK_DEV, 0).reshape(TOK_DEV, QUERY_HEADS, HEAD_SIZE)
        block_of_keys = lax.dynamic_slice_in_dim(padded_keys, row_begin, key_extent, 0).reshape(key_extent, KEY_VALUE_HEADS, HEAD_SIZE)
        block_of_values = lax.dynamic_slice_in_dim(padded_values, row_begin, key_extent, 0).reshape(key_extent, KEY_VALUE_HEADS, HEAD_SIZE)
        query_places = row_begin + jnp.arange(TOK_DEV, dtype=jnp.int32)
        key_places = row_begin - ATTEND_WINDOW + jnp.arange(key_extent, dtype=jnp.int32)
        gap_rows = query_places[:, None] - key_places[None, :]
        allowed = (gap_rows >= 0) & (gap_rows < ATTEND_WINDOW) & (key_places[None, :] >= 0)
        attn, grad_query, key_gradient, value_gradient = attend_block(query_block, grad_block, block_of_keys, block_of_values, allowed)
        key_accumulator = lax.dynamic_update_slice_in_dim(key_accumulator, lax.dynamic_slice_in_dim(key_accumulator, row_begin, key_extent, 0) + key_gradient.reshape(key_extent, KEY_VALUE_HEADS * HEAD_SIZE), row_begin, 0)
        value_accumulator = lax.dynamic_update_slice_in_dim(value_accumulator, lax.dynamic_slice_in_dim(value_accumulator, row_begin, key_extent, 0) + value_gradient.reshape(key_extent, KEY_VALUE_HEADS * HEAD_SIZE), row_begin, 0)
        return (key_accumulator, value_accumulator), (attn.reshape(TOK_DEV, QUERY_HEADS * HEAD_SIZE), grad_query.reshape(TOK_DEV, QUERY_HEADS * HEAD_SIZE))

    start_accumulator = jnp.zeros((SEQUENCE_TOKENS + ATTEND_WINDOW, KEY_VALUE_HEADS * HEAD_SIZE), jnp.float32)
    running, produced = lax.scan(block_step, (start_accumulator, start_accumulator), jnp.arange(SEQUENCE_TOKENS // TOK_DEV, dtype=jnp.int32))
    attn_rows = produced[0].reshape(SEQUENCE_TOKENS, QUERY_HEADS * HEAD_SIZE)
    query_grads = produced[1].reshape(SEQUENCE_TOKENS, QUERY_HEADS * HEAD_SIZE)
    key_grads = running[0][ATTEND_WINDOW:].astype(jnp.bfloat16)
    value_grads = running[1][ATTEND_WINDOW:].astype(jnp.bfloat16)
    return (place_rows(attn_rows, new_offsets), place_rows(query_grads, new_offsets), place_rows(key_grads, new_offsets), place_rows(value_grads, new_offsets))
```

```python
import functools

import jax
import jax.numpy as jnp
from jax import lax
from jax.experimental import pallas as pl
from jax.experimental.pallas import tpu as pltpu
from jax.sharding import PartitionSpec as P

TOK_DEV = 128
ATTEND_WINDOW = 1024
HEAD_SIZE = 128


query_scale = 168.0 ** (-0.5)


def shifted(value, axis, steps):
    count = lax.axis_size(axis)
    initial, last = (max(0, -steps), min(count, count - steps))
    return lax.ppermute(value, axis, [(source, source + steps) for source in range(initial, last)])


def relocate(row_data, source, target, slot_slack, out_rows):
    device = lax.axis_index("seq")
    own_rows = row_data.shape[0]
    first_row = source[device]
    end_row = source[device + 1]
    tail_start = jnp.maximum(end_row - first_row - slot_slack, 0)
    tail_rows = lax.dynamic_slice_in_dim(row_data, tail_start, slot_slack, 0)
    head_rows = row_data[:slot_slack]
    from_left = shifted(tail_rows, "seq", 1)
    from_right = shifted(head_rows, "seq", -1)
    before_row = source[jnp.maximum(device - 1, 0)]
    left_start = before_row + jnp.maximum(first_row - before_row - slot_slack, 0)
    candidates = jnp.concatenate([from_left, row_data, from_right], axis=0)
    targets = target[device] + jnp.arange(out_rows, dtype=jnp.int32)
    selected = jnp.where(
        targets < first_row,
        targets - left_start,
        jnp.where(
            targets < end_row,
            slot_slack + targets - first_row,
            slot_slack + own_rows + targets - end_row,
        ),
    )
    selected = jnp.clip(selected, 0, candidates.shape[0] - 1)
    is_live = targets < target[device + 1]
    return jnp.where(
        is_live[:, None], jnp.take(candidates, selected, axis=0), jnp.zeros((), row_data.dtype)
    )


def key_window(key_value, farthest, nearest):
    device = lax.axis_index("seq")
    devices = lax.axis_size("seq")
    gathered, places, live_parts = ([], [], [])
    for distance in range(farthest, nearest - 1, -1):
        if distance == 0:
            arrived = key_value
        else:
            arrived = shifted(key_value, "seq", distance)
        source_block = device - distance
        gathered.append(arrived)
        places.append(source_block * TOK_DEV + jnp.arange(TOK_DEV, dtype=jnp.int32))
        live_parts.append(jnp.full((TOK_DEV,), (source_block >= 0) & (source_block < devices)))
    return (jnp.concatenate(gathered, axis=0), jnp.concatenate(places), jnp.concatenate(live_parts))


def return_grads(grads, farthest, nearest):
    summed = None
    for position, distance in enumerate(range(farthest, nearest - 1, -1)):
        block = grads[position * TOK_DEV : (position + 1) * TOK_DEV]
        if distance == 0:
            arrived = block
        else:
            arrived = shifted(block, "seq", -distance)
        summed = arrived if summed is None else summed + arrived
    return summed


def attend(
    queries, grads_out, key_rows, value_rows, query_places, query_live, key_places, key_live
):
    head_count = queries.shape[1] // HEAD_SIZE
    kv_count = key_rows.shape[1] // HEAD_SIZE
    heads_per_group = head_count // kv_count
    gap_rows = query_places[:, None] - key_places[None, :]
    allowed = (gap_rows >= 0) & (gap_rows < ATTEND_WINDOW) & query_live[:, None] & key_live[None, :]
    contract_last = (((1,), (1,)), ((), ()))
    contract_first = (((0,), (0,)), ((), ()))
    attn_parts, query_grads, key_grads, value_grads = ([], [], [], [])
    for kv_head in range(kv_count):
        key_head = key_rows[:, kv_head * HEAD_SIZE : (kv_head + 1) * HEAD_SIZE]
        value_head = value_rows[:, kv_head * HEAD_SIZE : (kv_head + 1) * HEAD_SIZE]
        key_total = jnp.zeros((key_rows.shape[0], HEAD_SIZE), jnp.float32)
        value_total = jnp.zeros((key_rows.shape[0], HEAD_SIZE), jnp.float32)
        for member in range(heads_per_group):
            head_number = kv_head * heads_per_group + member
            query_head = queries[:, head_number * HEAD_SIZE : (head_number + 1) * HEAD_SIZE]
            grad_head = grads_out[:, head_number * HEAD_SIZE : (head_number + 1) * HEAD_SIZE]
            scores = (
                lax.dot_general(
                    query_head, key_head, contract_last, preferred_element_type=jnp.float32
                )
                * query_scale
            )
            scores = jnp.where(allowed, scores, -1e30)
            row_max = jnp.max(scores, axis=1, keepdims=True)
            weights = jnp.where(allowed, jnp.exp(scores - row_max), 0.0)
            row_total = jnp.sum(weights, axis=1, keepdims=True)
            probabilities = weights / jnp.where(query_live[:, None], row_total, 1.0)
            rounded = probabilities.astype(jnp.bfloat16)
            head_out = jnp.dot(rounded, value_head, preferred_element_type=jnp.float32).astype(
                jnp.bfloat16
            )
            row_delta = jnp.sum(
                grad_head.astype(jnp.float32) * head_out.astype(jnp.float32), axis=1, keepdims=True
            )
            grad_prob = lax.dot_general(
                grad_head, value_head, contract_last, preferred_element_type=jnp.float32
            )
            grad_score = (probabilities * (grad_prob - row_delta) * query_scale).astype(
                jnp.bfloat16
            )
            query_grads.append(
                jnp.dot(grad_score, key_head, preferred_element_type=jnp.float32).astype(
                    jnp.bfloat16
                )
            )
            key_total = key_total + lax.dot_general(
                grad_score, query_head, contract_first, preferred_element_type=jnp.float32
            )
            value_total = value_total + lax.dot_general(
                rounded, grad_head, contract_first, preferred_element_type=jnp.float32
            )
            attn_parts.append(head_out)
        key_grads.append(key_total)
        value_grads.append(value_total)
    return (
        jnp.concatenate(attn_parts, axis=1),
        jnp.concatenate(query_grads, axis=1),
        jnp.concatenate(key_grads, axis=1),
        jnp.concatenate(value_grads, axis=1),
    )


def on_device(q_old, k_old, value_old_layout, dout_old, old_offsets, new_offsets):
    query_rows, grad_rows, key_rows, value_rows = (
        lax.all_to_all(q_old, "head", split_axis=1, concat_axis=0, tiled=True),
        lax.all_to_all(dout_old, "head", split_axis=1, concat_axis=0, tiled=True),
        lax.all_to_all(k_old, "head", split_axis=1, concat_axis=0, tiled=True),
        lax.all_to_all(value_old_layout, "head", split_axis=1, concat_axis=0, tiled=True),
    )
    device = lax.axis_index("seq")
    devices = lax.axis_size("seq")
    even_offsets = jnp.arange(devices + 1, dtype=jnp.int32) * TOK_DEV
    query_width = query_rows.shape[1]
    key_width = key_rows.shape[1]
    slot_rows = query_rows.shape[0]
    slot_slack = (slot_rows - TOK_DEV) // 2
    halo_blocks = ATTEND_WINDOW // TOK_DEV
    relocated = relocate(
        jnp.concatenate([query_rows, grad_rows, key_rows, value_rows], axis=1),
        old_offsets,
        even_offsets,
        slot_slack,
        TOK_DEV,
    )
    queries = relocated[:, :query_width]
    grads_out = relocated[:, query_width : 2 * query_width]
    buffered, key_places, key_live = key_window(relocated[:, 2 * query_width :], halo_blocks, 0)
    query_places = device * TOK_DEV + jnp.arange(TOK_DEV, dtype=jnp.int32)
    query_live = jnp.full((TOK_DEV,), True)
    attn, grad_query, key_grad, value_grad = attend(
        queries,
        grads_out,
        buffered[:, :key_width],
        buffered[:, key_width:],
        query_places,
        query_live,
        key_places,
        key_live,
    )
    pair_grads = return_grads(
        jnp.concatenate([key_grad, value_grad], axis=1), halo_blocks, 0
    ).astype(jnp.bfloat16)
    placed = relocate(
        jnp.concatenate([attn, grad_query, pair_grads], axis=1),
        even_offsets,
        new_offsets,
        slot_slack,
        slot_rows,
    )
    attn_out = placed[:, :query_width]
    grad_query_out = placed[:, query_width : 2 * query_width]
    grad_key_out = placed[:, 2 * query_width : 2 * query_width + key_width]
    grad_value_out = placed[:, 2 * query_width + key_width :]
    return (attn_out, grad_query_out, grad_key_out, grad_value_out)


def joint_kernel(levels, pair, groups, members, *refs):
    (old_offsets, new_offsets, q_in, k_in, v_in, d_in, attn_out, dq_out, dk_out, dv_out,
     kv_chunks, qd_chunks, wide, kv_wide, qd_wide, kv_halo, qd_halo, keys, values, queries, grads,
     probs, grad_probs, grad_send, grad_recv, grad_own, attn_t, dq_t, row_buf, grad_buf, row_ext,
     grad_ext, in_send, in_recv, in_local, halo_send, halo_recv, cast_send, cast_recv, ret_send,
     ret_recv, out_send, out_recv, out_local) = refs
    seq, column = lax.axis_index("seq"), lax.axis_index("head")
    level, part = seq // pair, seq % pair
    crowd = pair * groups
    me = part * groups + column
    chunk = k_in.shape[0]
    slots = chunk * groups
    slack = (slots - TOK_DEV) // 2
    rows = pair * TOK_DEV
    width = members * HEAD_SIZE
    f32, bf16 = jnp.float32, jnp.bfloat16

    def at(to_level, to_part, to_column):
        return {"seq": to_level * pair + to_part, "head": to_column}

    def send(src, dst, ssem, rsem, where):
        return pltpu.make_async_remote_copy(
            src_ref=src, dst_ref=dst, send_sem=ssem, recv_sem=rsem, device_id=where,
            device_id_type=pl.DeviceIdType.MESH)

    here = at(level, part, column)

    def landed(dst, rsem):
        send(dst, dst, rsem, rsem, here).wait_recv()

    def left(src, ssem):
        send(src, src, ssem, ssem, here).wait_send()

    barrier = pltpu.get_barrier_semaphore()
    for step in range(1, crowd):
        peer = lax.rem(me + step, crowd)
        pl.semaphore_signal(barrier, inc=1, device_id=at(level, peer // groups, peer % groups),
                            device_id_type=pl.DeviceIdType.MESH)
    for step in range(1, levels):
        for other in range(pair):
            pl.semaphore_signal(barrier, inc=1, device_id=at(lax.rem(level + step, levels), other, column),
                                device_id_type=pl.DeviceIdType.MESH)
    pl.semaphore_wait(barrier, crowd - 1 + (levels - 1) * pair)

    def pieces(owner, source):
        head = (owner % groups) * pair + owner // groups
        k_at = pl.ds(pl.multiple_of(head * HEAD_SIZE, HEAD_SIZE), HEAD_SIZE)
        q_at = pl.ds(pl.multiple_of(head * width, HEAD_SIZE), width)
        return (
            (k_in.at[:, k_at], kv_chunks.at[source, :, pl.ds(0, HEAD_SIZE)]),
            (v_in.at[:, k_at], kv_chunks.at[source, :, pl.ds(HEAD_SIZE, HEAD_SIZE)]),
            (q_in.at[:, q_at], qd_chunks.at[source, :, pl.ds(0, width)]),
            (d_in.at[:, q_at], qd_chunks.at[source, :, pl.ds(width, width)]),
        )

    for kinds in ((0, 1), (2, 3)):
        for step in range(crowd):
            peer = lax.rem(me + step, crowd)
            for kind in kinds:
                src, dst = pieces(peer, me)[kind]
                if step == 0:
                    pltpu.make_async_copy(src, dst, in_local.at[kind]).start()
                else:
                    send(src, dst, in_send.at[kind, step], in_recv.at[kind, step],
                         at(level, peer // groups, peer % groups)).start()

    def arrive(kinds):
        for kind in kinds:
            src, dst = pieces(me, me)[kind]
            pltpu.make_async_copy(src, dst, in_local.at[kind]).wait()
            for step in range(1, crowd):
                source = lax.rem(me + crowd - step, crowd)
                landed(pieces(me, source)[kind][1], in_recv.at[kind, step])

    def spread(chunks, target):
        count = chunks.shape[2]
        wide[:, pl.ds(0, count)] = jnp.zeros((rows + 2 * slack, count), f32)
        row = lax.broadcasted_iota(jnp.int32, (slots, chunk), 0)
        slot = lax.broadcasted_iota(jnp.int32, (slots, chunk), 1)
        for other in range(pair):
            block = level * pair + other
            first, end = old_offsets[block], old_offsets[block + 1]
            total = jnp.zeros((slots, count), f32)
            for piece in range(groups):
                place = slot + (first + piece * chunk)
                pick = (row + (block * TOK_DEV - slack) == place) & (place < end)
                total = total + jnp.dot(jnp.where(pick, 1.0, 0.0).astype(bf16),
                                        chunks[other * groups + piece], preferred_element_type=f32)
            span = pl.ds(other * TOK_DEV, slots)
            wide[span, pl.ds(0, count)] = wide[span, pl.ds(0, count)] + total
        target[...] = wide[:, pl.ds(0, count)].astype(bf16)

    def halo(kind, source, dest):
        down = (source.at[pl.ds(0, slack)], dest.at[1])
        up = (source.at[pl.ds(rows + slack, slack)], dest.at[0])

        @pl.when(level > 0)
        def _():
            send(*down, halo_send.at[kind, 1], halo_recv.at[kind, 1], at(level - 1, part, column)).start()

        @pl.when(level < levels - 1)
        def _():
            send(*up, halo_send.at[kind, 0], halo_recv.at[kind, 0], at(level + 1, part, column)).start()

        @pl.when(level > 0)
        def _():
            landed(dest.at[0], halo_recv.at[kind, 0])

        @pl.when(level == 0)
        def _():
            dest[0] = jnp.zeros(dest.shape[1:], bf16)

        @pl.when(level < levels - 1)
        def _():
            landed(dest.at[1], halo_recv.at[kind, 1])

        @pl.when(level == levels - 1)
        def _():
            dest[1] = jnp.zeros(dest.shape[1:], bf16)

        return jnp.concatenate([
            source[pl.ds(slack, slack)] + dest[0],
            source[pl.ds(2 * slack, rows - 2 * slack)],
            source[pl.ds(rows, slack)] + dest[1],
        ], axis=0)

    arrive((0, 1))
    spread(kv_chunks, kv_wide)
    block = halo(0, kv_wide, kv_halo)
    keys[level] = block[:, :HEAD_SIZE]
    values[level] = block[:, HEAD_SIZE:]
    for kind, held in ((0, keys), (1, values)):
        for step in range(1, levels):
            @pl.when(level + step < levels)
            def _():
                send(held.at[level], held.at[level], cast_send.at[kind, step],
                     cast_recv.at[kind, step], at(level + step, part, column)).start()

    arrive((2, 3))
    spread(qd_chunks, qd_wide)
    block = halo(1, qd_wide, qd_halo)
    for member in range(members):
        span = pl.ds(member * rows, rows)
        queries[span] = block[:, member * HEAD_SIZE:(member + 1) * HEAD_SIZE]
        grads[span] = block[:, width + member * HEAD_SIZE:width + (member + 1) * HEAD_SIZE]

    nt = (((1,), (1,)), ((), ()))
    tn = (((0,), (0,)), ((), ()))
    lanes = members * rows

    def score_step(step, row_max):
        @pl.when(step > 0)
        def _():
            landed(keys.at[level - step], cast_recv.at[0, step])

        score = lax.dot_general(keys[level - step], queries[...], nt, preferred_element_type=f32) * query_scale
        key_place = lax.broadcasted_iota(jnp.int32, (rows, rows), 0)
        query_place = lax.broadcasted_iota(jnp.int32, (rows, rows), 1) + step * rows
        allowed = jnp.concatenate([key_place <= query_place] * members, axis=1)
        score = jnp.where(allowed, score, -1e30)
        probs[level - step] = score
        return jnp.maximum(row_max, jnp.max(score, axis=0, keepdims=True))

    row_max = lax.fori_loop(0, level + 1, score_step, jnp.full((1, lanes), -1e30, f32))

    def weight_step(step, total):
        weight = jnp.exp(probs[step] - row_max)
        probs[step] = weight
        return total + jnp.sum(weight, axis=0, keepdims=True)

    row_total = lax.fori_loop(0, level + 1, weight_step, jnp.zeros((1, lanes), f32))
    inverse = 1.0 / row_total
    attn_t[...] = jnp.zeros_like(attn_t)

    def value_step(step, carry):
        @pl.when(step > 0)
        def _():
            landed(values.at[level - step], cast_recv.at[1, step])

        prob = probs[level - step] * inverse
        probs[level - step] = prob
        attn_t[...] += lax.dot_general(values[level - step], prob.astype(bf16), tn, preferred_element_type=f32)
        grad_probs[level - step] = lax.dot_general(values[level - step], grads[...], nt, preferred_element_type=f32)
        return carry

    lax.fori_loop(0, level + 1, value_step, 0)
    attn = attn_t[...].astype(bf16).astype(f32)
    delta = jnp.sum(attn * jnp.transpose(grads[...].astype(f32)), axis=0, keepdims=True)
    attn = jnp.transpose(attn).astype(bf16)
    dq_t[...] = jnp.zeros_like(dq_t)

    def grad_step(low, carry):
        prob = probs[low]
        change = (prob * (grad_probs[low] - delta) * query_scale).astype(bf16)
        dq_t[...] += lax.dot_general(keys[low], change, tn, preferred_element_type=f32)
        dk = jnp.dot(change, queries[...], preferred_element_type=f32)
        dv = jnp.dot(prob.astype(bf16), grads[...], preferred_element_type=f32)

        @pl.when(low < level)
        def _():
            grad_send[low] = jnp.concatenate([dk, dv], axis=1).astype(bf16)
            send(grad_send.at[low], grad_recv.at[level - low], ret_send.at[level - low],
                 ret_recv.at[level - low], at(low, part, column)).start()

        @pl.when(low == level)
        def _():
            grad_own[...] = jnp.concatenate([dk, dv], axis=1)

        return carry

    lax.fori_loop(0, level + 1, grad_step, 0)
    dq = jnp.transpose(dq_t[...]).astype(bf16)
    for member in range(members):
        span = slice(member * rows, (member + 1) * rows)
        row_buf[:, pl.ds(member * HEAD_SIZE, HEAD_SIZE)] = attn[span]
        row_buf[:, pl.ds(width + member * HEAD_SIZE, HEAD_SIZE)] = dq[span]

    def routes(other):
        begin = other * TOK_DEV - slack
        low, high = max(0, begin), min(rows, begin + slots)
        return pl.ds(low, high - low), pl.ds(low - begin, high - low)

    head_span, tail_span = pl.ds(0, slack), pl.ds(slots - slack, slack)
    last_span = pl.ds(rows - slack, slack)

    def hand_out(kind, source, dest):
        for other in range(pair):
            take, put = routes(other)

            @pl.when(part == other)
            def _():
                pltpu.make_async_copy(source.at[take], dest.at[part, put], out_local.at[kind]).start()

            @pl.when(part != other)
            def _():
                send(source.at[take], dest.at[part, put], out_send.at[kind, other],
                     out_recv.at[kind, part, 0], at(level, other, column)).start()

        @pl.when(level < levels - 1)
        def _():
            send(source.at[last_span], dest.at[part, head_span], out_send.at[kind, pair],
                 out_recv.at[kind, part, 1], at(level + 1, 0, column)).start()

        @pl.when(level > 0)
        def _():
            send(source.at[head_span], dest.at[part, tail_span], out_send.at[kind, pair + 1],
                 out_recv.at[kind, part, 2], at(level - 1, pair - 1, column)).start()

    def take_in(kind, source, dest, place):
        for other in range(pair):
            take, put = routes(other)

            @pl.when(part == other)
            def _():
                pltpu.make_async_copy(source.at[take], dest.at[part, put], out_local.at[kind]).wait()
                for giver in range(pair):
                    if giver != other:
                        landed(dest.at[giver, put], out_recv.at[kind, giver, 0])

            @pl.when(part != other)
            def _():
                left(source.at[take], out_send.at[kind, other])

        for giver in range(pair):
            @pl.when((part == 0) & (level > 0))
            def _():
                landed(dest.at[giver, head_span], out_recv.at[kind, giver, 1])

            @pl.when((part == 0) & (level == 0))
            def _():
                dest[giver, head_span] = jnp.zeros((slack, dest.shape[2]), bf16)

            @pl.when((part == pair - 1) & (level < levels - 1))
            def _():
                landed(dest.at[giver, tail_span], out_recv.at[kind, giver, 2])

            @pl.when((part == pair - 1) & (level == levels - 1))
            def _():
                dest[giver, tail_span] = jnp.zeros((slack, dest.shape[2]), bf16)

        @pl.when(level < levels - 1)
        def _():
            left(source.at[last_span], out_send.at[kind, pair])

        @pl.when(level > 0)
        def _():
            left(source.at[head_span], out_send.at[kind, pair + 1])

        first, end = new_offsets[seq], new_offsets[seq + 1]
        slot = lax.broadcasted_iota(jnp.int32, (slots, slots), 0) + first
        held = lax.broadcasted_iota(jnp.int32, (slots, slots), 1) + (seq * TOK_DEV - slack)
        pick = jnp.where((slot == held) & (slot < end), 1.0, 0.0).astype(bf16)
        for giver in range(pair):
            placed = jnp.dot(pick, dest[giver], preferred_element_type=f32).astype(bf16)
            for index, out in enumerate(place):
                count = dest.shape[2] // 2
                out[:, pl.ds(giver * count, count)] = placed[:, index * count:(index + 1) * count]

    hand_out(0, row_buf, row_ext)
    for step in range(1, levels):
        @pl.when(level + step < levels)
        def _():
            landed(grad_recv.at[step], ret_recv.at[step])
            grad_own[...] += grad_recv[step].astype(f32)
    grad_buf[...] = grad_own[...].astype(bf16)
    hand_out(1, grad_buf, grad_ext)
    take_in(0, row_buf, row_ext, (attn_out, dq_out))
    take_in(1, grad_buf, grad_ext, (dk_out, dv_out))

    for kind in range(4):
        for step in range(1, crowd):
            left(pieces(me, me)[kind][0], in_send.at[kind, step])
    for kind, source in ((0, kv_wide), (1, qd_wide)):
        @pl.when(level > 0)
        def _():
            left(source.at[pl.ds(0, slack)], halo_send.at[kind, 1])

        @pl.when(level < levels - 1)
        def _():
            left(source.at[pl.ds(rows + slack, slack)], halo_send.at[kind, 0])
    for step in range(1, levels):
        for kind, held in ((0, keys), (1, values)):
            @pl.when(level + step < levels)
            def _():
                left(held.at[level], cast_send.at[kind, step])

        @pl.when(level >= step)
        def _():
            left(grad_send.at[level - step], ret_send.at[step])


def joint(sequence, groups, q_old, k_old, value_old_layout, dout_old, old_offsets, new_offsets):
    chunk = q_old.shape[0]
    pair = k_old.shape[1] // (groups * HEAD_SIZE)
    members = q_old.shape[1] // k_old.shape[1]
    levels = sequence // pair
    slots = chunk * groups
    slack = (slots - TOK_DEV) // 2
    rows = pair * TOK_DEV
    width = members * HEAD_SIZE
    lanes = members * rows
    bf16, f32 = jnp.bfloat16, jnp.float32
    vmem, dma = pltpu.VMEM, pltpu.SemaphoreType.DMA
    out = lambda count: jax.ShapeDtypeStruct((slots, count), bf16)
    smem = pl.BlockSpec(memory_space=pltpu.SMEM)
    anywhere = pl.BlockSpec(memory_space=pl.ANY)
    whole = pl.BlockSpec(memory_space=pltpu.VMEM)
    return pl.pallas_call(
        functools.partial(joint_kernel, levels, pair, groups, members),
        out_shape=(out(pair * width), out(pair * width), out(pair * HEAD_SIZE), out(pair * HEAD_SIZE)),
        in_specs=[smem, smem, anywhere, anywhere, anywhere, anywhere],
        out_specs=(whole,) * 4,
        scratch_shapes=[
            vmem((pair * groups, chunk, 2 * HEAD_SIZE), bf16),
            vmem((pair * groups, chunk, 2 * width), bf16),
            vmem((rows + 2 * slack, 2 * width), f32),
            vmem((rows + 2 * slack, 2 * HEAD_SIZE), bf16),
            vmem((rows + 2 * slack, 2 * width), bf16),
            vmem((2, slack, 2 * HEAD_SIZE), bf16),
            vmem((2, slack, 2 * width), bf16),
            vmem((levels, rows, HEAD_SIZE), bf16),
            vmem((levels, rows, HEAD_SIZE), bf16),
            vmem((lanes, HEAD_SIZE), bf16),
            vmem((lanes, HEAD_SIZE), bf16),
            vmem((levels, rows, lanes), f32),
            vmem((levels, rows, lanes), f32),
            vmem((levels, rows, 2 * HEAD_SIZE), bf16),
            vmem((levels, rows, 2 * HEAD_SIZE), bf16),
            vmem((rows, 2 * HEAD_SIZE), f32),
            vmem((HEAD_SIZE, lanes), f32),
            vmem((HEAD_SIZE, lanes), f32),
            vmem((rows, 2 * width), bf16),
            vmem((rows, 2 * HEAD_SIZE), bf16),
            vmem((pair, slots, 2 * width), bf16),
            vmem((pair, slots, 2 * HEAD_SIZE), bf16),
            dma((4, pair * groups)), dma((4, pair * groups)), dma((4,)),
            dma((2, 2)), dma((2, 2)),
            dma((2, levels)), dma((2, levels)),
            dma((levels,)), dma((levels,)),
            dma((2, pair + 2)), dma((2, pair, 3)), dma((2,)),
        ],
        compiler_params=pltpu.CompilerParams(collective_id=0, has_side_effects=True),
    )(old_offsets, new_offsets, q_old, k_old, value_old_layout, dout_old)


def solution(mesh):
    sequence, groups = mesh.shape["seq"], mesh.shape["head"]
    covered = sequence * TOK_DEV <= ATTEND_WINDOW
    body = functools.partial(joint, sequence, groups) if covered else on_device
    return jax.shard_map(
        body,
        mesh=mesh,
        in_specs=(
            P(("seq", "head"), None),
            P(("seq", "head"), None),
            P(("seq", "head"), None),
            P(("seq", "head"), None),
            P(),
            P(),
        ),
        out_specs=(P("seq", "head"), P("seq", "head"), P("seq", "head"), P("seq", "head")),
        check_vma=False,
    )
```

```python
import functools

import jax
import jax.numpy as jnp
from jax import lax
from jax.experimental import pallas as pl
from jax.experimental.pallas import tpu as pltpu
from jax.sharding import PartitionSpec as P

TOK_DEV = 128
ATTEND_WINDOW = 1024
HEAD_SIZE = 128


query_scale = 168.0 ** (-0.5)


def shifted(value, axis, steps):
    count = lax.axis_size(axis)
    initial, last = (max(0, -steps), min(count, count - steps))
    return lax.ppermute(value, axis, [(source, source + steps) for source in range(initial, last)])


def relocate(row_data, source, target, slot_slack, out_rows):
    device = lax.axis_index("seq")
    own_rows = row_data.shape[0]
    first_row = source[device]
    end_row = source[device + 1]
    tail_start = jnp.maximum(end_row - first_row - slot_slack, 0)
    tail_rows = lax.dynamic_slice_in_dim(row_data, tail_start, slot_slack, 0)
    head_rows = row_data[:slot_slack]
    from_left = shifted(tail_rows, "seq", 1)
    from_right = shifted(head_rows, "seq", -1)
    before_row = source[jnp.maximum(device - 1, 0)]
    left_start = before_row + jnp.maximum(first_row - before_row - slot_slack, 0)
    candidates = jnp.concatenate([from_left, row_data, from_right], axis=0)
    targets = target[device] + jnp.arange(out_rows, dtype=jnp.int32)
    selected = jnp.where(
        targets < first_row,
        targets - left_start,
        jnp.where(
            targets < end_row,
            slot_slack + targets - first_row,
            slot_slack + own_rows + targets - end_row,
        ),
    )
    selected = jnp.clip(selected, 0, candidates.shape[0] - 1)
    is_live = targets < target[device + 1]
    return jnp.where(
        is_live[:, None], jnp.take(candidates, selected, axis=0), jnp.zeros((), row_data.dtype)
    )


def key_window(key_value, farthest, nearest):
    device = lax.axis_index("seq")
    devices = lax.axis_size("seq")
    gathered, places, live_parts = ([], [], [])
    for distance in range(farthest, nearest - 1, -1):
        if distance == 0:
            arrived = key_value
        else:
            arrived = shifted(key_value, "seq", distance)
        source_block = device - distance
        gathered.append(arrived)
        places.append(source_block * TOK_DEV + jnp.arange(TOK_DEV, dtype=jnp.int32))
        live_parts.append(jnp.full((TOK_DEV,), (source_block >= 0) & (source_block < devices)))
    return (jnp.concatenate(gathered, axis=0), jnp.concatenate(places), jnp.concatenate(live_parts))


def return_grads(grads, farthest, nearest):
    summed = None
    for position, distance in enumerate(range(farthest, nearest - 1, -1)):
        block = grads[position * TOK_DEV : (position + 1) * TOK_DEV]
        if distance == 0:
            arrived = block
        else:
            arrived = shifted(block, "seq", -distance)
        summed = arrived if summed is None else summed + arrived
    return summed


def attend(
    queries, grads_out, key_rows, value_rows, query_places, query_live, key_places, key_live
):
    head_count = queries.shape[1] // HEAD_SIZE
    kv_count = key_rows.shape[1] // HEAD_SIZE
    heads_per_group = head_count // kv_count
    gap_rows = query_places[:, None] - key_places[None, :]
    allowed = (gap_rows >= 0) & (gap_rows < ATTEND_WINDOW) & query_live[:, None] & key_live[None, :]
    contract_last = (((1,), (1,)), ((), ()))
    contract_first = (((0,), (0,)), ((), ()))
    attn_parts, query_grads, key_grads, value_grads = ([], [], [], [])
    for kv_head in range(kv_count):
        key_head = key_rows[:, kv_head * HEAD_SIZE : (kv_head + 1) * HEAD_SIZE]
        value_head = value_rows[:, kv_head * HEAD_SIZE : (kv_head + 1) * HEAD_SIZE]
        key_total = jnp.zeros((key_rows.shape[0], HEAD_SIZE), jnp.float32)
        value_total = jnp.zeros((key_rows.shape[0], HEAD_SIZE), jnp.float32)
        for member in range(heads_per_group):
            head_number = kv_head * heads_per_group + member
            query_head = queries[:, head_number * HEAD_SIZE : (head_number + 1) * HEAD_SIZE]
            grad_head = grads_out[:, head_number * HEAD_SIZE : (head_number + 1) * HEAD_SIZE]
            scores = (
                lax.dot_general(
                    query_head, key_head, contract_last, preferred_element_type=jnp.float32
                )
                * query_scale
            )
            scores = jnp.where(allowed, scores, -1e30)
            row_max = jnp.max(scores, axis=1, keepdims=True)
            weights = jnp.where(allowed, jnp.exp(scores - row_max), 0.0)
            row_total = jnp.sum(weights, axis=1, keepdims=True)
            probabilities = weights / jnp.where(query_live[:, None], row_total, 1.0)
            rounded = probabilities.astype(jnp.bfloat16)
            head_out = jnp.dot(rounded, value_head, preferred_element_type=jnp.float32).astype(
                jnp.bfloat16
            )
            row_delta = jnp.sum(
                grad_head.astype(jnp.float32) * head_out.astype(jnp.float32), axis=1, keepdims=True
            )
            grad_prob = lax.dot_general(
                grad_head, value_head, contract_last, preferred_element_type=jnp.float32
            )
            grad_score = (probabilities * (grad_prob - row_delta) * query_scale).astype(
                jnp.bfloat16
            )
            query_grads.append(
                jnp.dot(grad_score, key_head, preferred_element_type=jnp.float32).astype(
                    jnp.bfloat16
                )
            )
            key_total = key_total + lax.dot_general(
                grad_score, query_head, contract_first, preferred_element_type=jnp.float32
            )
            value_total = value_total + lax.dot_general(
                rounded, grad_head, contract_first, preferred_element_type=jnp.float32
            )
            attn_parts.append(head_out)
        key_grads.append(key_total)
        value_grads.append(value_total)
    return (
        jnp.concatenate(attn_parts, axis=1),
        jnp.concatenate(query_grads, axis=1),
        jnp.concatenate(key_grads, axis=1),
        jnp.concatenate(value_grads, axis=1),
    )


def on_device(q_old, k_old, value_old_layout, dout_old, old_offsets, new_offsets):
    query_rows, grad_rows, key_rows, value_rows = (
        lax.all_to_all(q_old, "head", split_axis=1, concat_axis=0, tiled=True),
        lax.all_to_all(dout_old, "head", split_axis=1, concat_axis=0, tiled=True),
        lax.all_to_all(k_old, "head", split_axis=1, concat_axis=0, tiled=True),
        lax.all_to_all(value_old_layout, "head", split_axis=1, concat_axis=0, tiled=True),
    )
    device = lax.axis_index("seq")
    devices = lax.axis_size("seq")
    even_offsets = jnp.arange(devices + 1, dtype=jnp.int32) * TOK_DEV
    query_width = query_rows.shape[1]
    key_width = key_rows.shape[1]
    slot_rows = query_rows.shape[0]
    slot_slack = (slot_rows - TOK_DEV) // 2
    halo_blocks = ATTEND_WINDOW // TOK_DEV
    relocated = relocate(
        jnp.concatenate([query_rows, grad_rows, key_rows, value_rows], axis=1),
        old_offsets,
        even_offsets,
        slot_slack,
        TOK_DEV,
    )
    queries = relocated[:, :query_width]
    grads_out = relocated[:, query_width : 2 * query_width]
    buffered, key_places, key_live = key_window(relocated[:, 2 * query_width :], halo_blocks, 0)
    query_places = device * TOK_DEV + jnp.arange(TOK_DEV, dtype=jnp.int32)
    query_live = jnp.full((TOK_DEV,), True)
    attn, grad_query, key_grad, value_grad = attend(
        queries,
        grads_out,
        buffered[:, :key_width],
        buffered[:, key_width:],
        query_places,
        query_live,
        key_places,
        key_live,
    )
    pair_grads = return_grads(
        jnp.concatenate([key_grad, value_grad], axis=1), halo_blocks, 0
    ).astype(jnp.bfloat16)
    placed = relocate(
        jnp.concatenate([attn, grad_query, pair_grads], axis=1),
        even_offsets,
        new_offsets,
        slot_slack,
        slot_rows,
    )
    attn_out = placed[:, :query_width]
    grad_query_out = placed[:, query_width : 2 * query_width]
    grad_key_out = placed[:, 2 * query_width : 2 * query_width + key_width]
    grad_value_out = placed[:, 2 * query_width + key_width :]
    return (attn_out, grad_query_out, grad_key_out, grad_value_out)


def joint_kernel(levels, pair, groups, members, *refs):
    (old_offsets, q_in, k_in, v_in, d_in, row_ext, dk_ext, dv_ext,
     kv_chunks, qd_chunks, wide, kv_wide, qd_wide, kv_halo, qd_halo, keys, values, queries, grads,
     probs, grad_probs, grad_send, grad_recv, grad_own, attn_t, dq_t, row_buf, grad_buf, in_send, in_recv, in_local, halo_send, halo_recv, cast_send, cast_recv, ret_send,
     ret_recv, out_send, out_recv, out_local) = refs
    seq, column = lax.axis_index("seq"), lax.axis_index("head")
    level, part = seq // pair, seq % pair
    crowd = pair * groups
    me = part * groups + column
    chunk = k_in.shape[0]
    slots = chunk * groups
    slack = (slots - TOK_DEV) // 2
    rows = pair * TOK_DEV
    width = members * HEAD_SIZE
    f32, bf16 = jnp.float32, jnp.bfloat16

    def at(to_level, to_part, to_column):
        return {"seq": to_level * pair + to_part, "head": to_column}

    def send(src, dst, ssem, rsem, where):
        return pltpu.make_async_remote_copy(
            src_ref=src, dst_ref=dst, send_sem=ssem, recv_sem=rsem, device_id=where,
            device_id_type=pl.DeviceIdType.MESH)

    here = at(level, part, column)

    def landed(dst, rsem):
        send(dst, dst, rsem, rsem, here).wait_recv()

    def left(src, ssem):
        send(src, src, ssem, ssem, here).wait_send()

    barrier = pltpu.get_barrier_semaphore()
    for step in range(1, crowd):
        peer = lax.rem(me + step, crowd)
        pl.semaphore_signal(barrier, inc=1, device_id=at(level, peer // groups, peer % groups),
                            device_id_type=pl.DeviceIdType.MESH)
    for step in range(1, levels):
        for other in range(pair):
            pl.semaphore_signal(barrier, inc=1, device_id=at(lax.rem(level + step, levels), other, column),
                                device_id_type=pl.DeviceIdType.MESH)
    pl.semaphore_wait(barrier, crowd - 1 + (levels - 1) * pair)

    def pieces(owner, source):
        head = (owner % groups) * pair + owner // groups
        k_at = pl.ds(pl.multiple_of(head * HEAD_SIZE, HEAD_SIZE), HEAD_SIZE)
        q_at = pl.ds(pl.multiple_of(head * width, HEAD_SIZE), width)
        return (
            (k_in.at[:, k_at], kv_chunks.at[source, :, pl.ds(0, HEAD_SIZE)]),
            (v_in.at[:, k_at], kv_chunks.at[source, :, pl.ds(HEAD_SIZE, HEAD_SIZE)]),
            (q_in.at[:, q_at], qd_chunks.at[source, :, pl.ds(0, width)]),
            (d_in.at[:, q_at], qd_chunks.at[source, :, pl.ds(width, width)]),
        )

    for kinds in ((0, 1), (2, 3)):
        for step in range(crowd):
            peer = lax.rem(me + step, crowd)
            for kind in kinds:
                src, dst = pieces(peer, me)[kind]
                if step == 0:
                    pltpu.make_async_copy(src, dst, in_local.at[kind]).start()
                else:
                    send(src, dst, in_send.at[kind, step], in_recv.at[kind, step],
                         at(level, peer // groups, peer % groups)).start()

    def arrive(kinds):
        for kind in kinds:
            src, dst = pieces(me, me)[kind]
            pltpu.make_async_copy(src, dst, in_local.at[kind]).wait()
            for step in range(1, crowd):
                source = lax.rem(me + crowd - step, crowd)
                landed(pieces(me, source)[kind][1], in_recv.at[kind, step])

    def spread(chunks, target):
        count = chunks.shape[2]
        wide[:, pl.ds(0, count)] = jnp.zeros((rows + 2 * slack, count), f32)
        row = lax.broadcasted_iota(jnp.int32, (slots, chunk), 0)
        slot = lax.broadcasted_iota(jnp.int32, (slots, chunk), 1)
        for other in range(pair):
            block = level * pair + other
            first, end = old_offsets[block], old_offsets[block + 1]
            total = jnp.zeros((slots, count), f32)
            for piece in range(groups):
                place = slot + (first + piece * chunk)
                pick = (row + (block * TOK_DEV - slack) == place) & (place < end)
                total = total + jnp.dot(jnp.where(pick, 1.0, 0.0).astype(bf16),
                                        chunks[other * groups + piece], preferred_element_type=f32)
            span = pl.ds(other * TOK_DEV, slots)
            wide[span, pl.ds(0, count)] = wide[span, pl.ds(0, count)] + total
        target[...] = wide[:, pl.ds(0, count)].astype(bf16)

    def halo(kind, source, dest):
        down = (source.at[pl.ds(0, slack)], dest.at[1])
        up = (source.at[pl.ds(rows + slack, slack)], dest.at[0])

        @pl.when(level > 0)
        def _():
            send(*down, halo_send.at[kind, 1], halo_recv.at[kind, 1], at(level - 1, part, column)).start()

        @pl.when(level < levels - 1)
        def _():
            send(*up, halo_send.at[kind, 0], halo_recv.at[kind, 0], at(level + 1, part, column)).start()

        def finish():
            @pl.when(level > 0)
            def _():
                landed(dest.at[0], halo_recv.at[kind, 0])

            @pl.when(level == 0)
            def _():
                dest[0] = jnp.zeros(dest.shape[1:], bf16)

            @pl.when(level < levels - 1)
            def _():
                landed(dest.at[1], halo_recv.at[kind, 1])

            @pl.when(level == levels - 1)
            def _():
                dest[1] = jnp.zeros(dest.shape[1:], bf16)

            return jnp.concatenate([
                source[pl.ds(slack, slack)] + dest[0],
                source[pl.ds(2 * slack, rows - 2 * slack)],
                source[pl.ds(rows, slack)] + dest[1],
            ], axis=0)

        return finish

    arrive((0, 1))
    spread(kv_chunks, kv_wide)
    block = halo(0, kv_wide, kv_halo)()
    keys[level] = block[:, :HEAD_SIZE]
    values[level] = block[:, HEAD_SIZE:]

    def forward(step):
        @pl.when(level < levels - 1)
        def _():
            send(keys.at[level - step], keys.at[level - step], cast_send.at[0, step],
                 cast_recv.at[0, step + 1], at(level + 1, part, column)).start()

    forward(0)
    if levels > 1:
        @pl.when(level > 0)
        def _():
            landed(keys.at[level - 1], cast_recv.at[0, 1])
            forward(1)

    arrive((2, 3))
    spread(qd_chunks, qd_wide)
    finish = halo(1, qd_wide, qd_halo)
    for step in range(1, levels):
        @pl.when(level + step < levels)
        def _():
            send(values.at[level], values.at[level], cast_send.at[1, step],
                 cast_recv.at[1, step], at(level + step, part, column)).start()
    block = finish()
    for member in range(members):
        span = pl.ds(member * rows, rows)
        queries[span] = block[:, member * HEAD_SIZE:(member + 1) * HEAD_SIZE]
        grads[span] = block[:, width + member * HEAD_SIZE:width + (member + 1) * HEAD_SIZE]

    nt = (((1,), (1,)), ((), ()))
    tn = (((0,), (0,)), ((), ()))
    lanes = members * rows

    def score_step(step, row_max):
        @pl.when(step > 1)
        def _():
            landed(keys.at[level - step], cast_recv.at[0, step])
            forward(step)

        score = lax.dot_general(keys[level - step], queries[...], nt, preferred_element_type=f32) * query_scale
        key_place = lax.broadcasted_iota(jnp.int32, (rows, rows), 0)
        query_place = lax.broadcasted_iota(jnp.int32, (rows, rows), 1) + step * rows
        allowed = jnp.concatenate([key_place <= query_place] * members, axis=1)
        score = jnp.where(allowed, score, -1e30)
        probs[level - step] = score
        return jnp.maximum(row_max, jnp.max(score, axis=0, keepdims=True))

    row_max = lax.fori_loop(0, level + 1, score_step, jnp.full((1, lanes), -1e30, f32))

    def weight_step(step, total):
        weight = jnp.exp(probs[step] - row_max)
        probs[step] = weight
        return total + jnp.sum(weight, axis=0, keepdims=True)

    row_total = lax.fori_loop(0, level + 1, weight_step, jnp.zeros((1, lanes), f32))
    inverse = 1.0 / row_total

    def share(kind, low, term):
        @pl.when(low < level)
        def _():
            grad_send[kind, low] = term.astype(bf16)
            send(grad_send.at[kind, low], grad_recv.at[kind, level - low], ret_send.at[kind, level - low],
                 ret_recv.at[kind, level - low], at(low, part, column)).start()

        @pl.when(low == level)
        def _():
            grad_own[kind] = term

    def prob_step(low, carry):
        prob = probs[low] * inverse
        probs[low] = prob
        share(0, low, jnp.dot(prob.astype(bf16), grads[...], preferred_element_type=f32))
        return carry

    lax.fori_loop(0, level + 1, prob_step, 0)
    attn_t[...] = jnp.zeros_like(attn_t)

    def value_step(step, carry):
        @pl.when(step > 0)
        def _():
            landed(values.at[level - step], cast_recv.at[1, step])

        prob = probs[level - step].astype(bf16)
        attn_t[...] += lax.dot_general(values[level - step], prob, tn, preferred_element_type=f32)
        grad_probs[level - step] = lax.dot_general(values[level - step], grads[...], nt, preferred_element_type=f32)
        return carry

    lax.fori_loop(0, level + 1, value_step, 0)
    attn = attn_t[...].astype(bf16).astype(f32)
    delta = jnp.sum(attn * jnp.transpose(grads[...].astype(f32)), axis=0, keepdims=True)
    attn = jnp.transpose(attn).astype(bf16)
    dq_t[...] = jnp.zeros_like(dq_t)

    def grad_step(low, carry):
        prob = probs[low]
        change = (prob * (grad_probs[low] - delta) * query_scale).astype(bf16)
        dq_t[...] += lax.dot_general(keys[low], change, tn, preferred_element_type=f32)
        share(1, low, jnp.dot(change, queries[...], preferred_element_type=f32))
        return carry

    lax.fori_loop(0, level + 1, grad_step, 0)
    dq = jnp.transpose(dq_t[...]).astype(bf16)
    for member in range(members):
        span = slice(member * rows, (member + 1) * rows)
        row_buf[:, pl.ds(member * HEAD_SIZE, HEAD_SIZE)] = attn[span]
        row_buf[:, pl.ds(width + member * HEAD_SIZE, HEAD_SIZE)] = dq[span]

    def routes(other):
        begin = other * TOK_DEV - slack
        low, high = max(0, begin), min(rows, begin + slots)
        return pl.ds(low, high - low), pl.ds(low - begin, high - low)

    head_span, tail_span = pl.ds(0, slack), pl.ds(slots - slack, slack)
    last_span = pl.ds(rows - slack, slack)

    def hand_out(kind, source, dest):
        for other in range(pair):
            take, put = routes(other)

            @pl.when(part == other)
            def _():
                pltpu.make_async_copy(source.at[take], dest.at[part, put], out_local.at[kind]).start()

            @pl.when(part != other)
            def _():
                send(source.at[take], dest.at[part, put], out_send.at[kind, other],
                     out_recv.at[kind, part, 0], at(level, other, column)).start()

        @pl.when(level < levels - 1)
        def _():
            send(source.at[last_span], dest.at[part, head_span], out_send.at[kind, pair],
                 out_recv.at[kind, part, 1], at(level + 1, 0, column)).start()

        @pl.when(level > 0)
        def _():
            send(source.at[head_span], dest.at[part, tail_span], out_send.at[kind, pair + 1],
                 out_recv.at[kind, part, 2], at(level - 1, pair - 1, column)).start()

    def take_in(kind, source, dest):
        for other in range(pair):
            take, put = routes(other)

            @pl.when(part == other)
            def _():
                pltpu.make_async_copy(source.at[take], dest.at[part, put], out_local.at[kind]).wait()
                for giver in range(pair):
                    if giver != other:
                        landed(dest.at[giver, put], out_recv.at[kind, giver, 0])

            @pl.when(part != other)
            def _():
                left(source.at[take], out_send.at[kind, other])

        for giver in range(pair):
            @pl.when((part == 0) & (level > 0))
            def _():
                landed(dest.at[giver, head_span], out_recv.at[kind, giver, 1])

            @pl.when((part == 0) & (level == 0))
            def _():
                dest[giver, head_span] = jnp.zeros((slack, dest.shape[2]), bf16)

            @pl.when((part == pair - 1) & (level < levels - 1))
            def _():
                landed(dest.at[giver, tail_span], out_recv.at[kind, giver, 2])

            @pl.when((part == pair - 1) & (level == levels - 1))
            def _():
                dest[giver, tail_span] = jnp.zeros((slack, dest.shape[2]), bf16)

        @pl.when(level < levels - 1)
        def _():
            left(source.at[last_span], out_send.at[kind, pair])

        @pl.when(level > 0)
        def _():
            left(source.at[head_span], out_send.at[kind, pair + 1])

    hand_out(0, row_buf, row_ext)
    for kind, dest in ((0, dv_ext), (1, dk_ext)):
        for step in range(1, levels):
            @pl.when(level + step < levels)
            def _():
                landed(grad_recv.at[kind, step], ret_recv.at[kind, step])
                grad_own[kind] += grad_recv[kind, step].astype(f32)
        grad_buf[kind] = grad_own[kind].astype(bf16)
        hand_out(1 + kind, grad_buf.at[kind], dest)
    take_in(0, row_buf, row_ext)
    take_in(1, grad_buf.at[0], dv_ext)
    take_in(2, grad_buf.at[1], dk_ext)

    for kind in range(4):
        for step in range(1, crowd):
            left(pieces(me, me)[kind][0], in_send.at[kind, step])
    for kind, source in ((0, kv_wide), (1, qd_wide)):
        @pl.when(level > 0)
        def _():
            left(source.at[pl.ds(0, slack)], halo_send.at[kind, 1])

        @pl.when(level < levels - 1)
        def _():
            left(source.at[pl.ds(rows + slack, slack)], halo_send.at[kind, 0])
    for step in range(1, levels):
        @pl.when(level + step < levels)
        def _():
            left(values.at[level], cast_send.at[1, step])

        @pl.when((level < levels - 1) & (level >= step - 1))
        def _():
            left(keys.at[level - step + 1], cast_send.at[0, step - 1])

        @pl.when(level >= step)
        def _():
            for kind in range(2):
                left(grad_send.at[kind, level - step], ret_send.at[kind, step])


def place_kernel(new_offsets, row_ext, dk_ext, dv_ext, attn_out, dq_out, dk_out, dv_out):
    seq = lax.axis_index("seq")
    pair, slots, width = row_ext.shape
    slack = (slots - TOK_DEV) // 2
    first, end = new_offsets[seq], new_offsets[seq + 1]
    slot = lax.broadcasted_iota(jnp.int32, (slots, slots), 0) + first
    held = lax.broadcasted_iota(jnp.int32, (slots, slots), 1) + (seq * TOK_DEV - slack)
    pick = jnp.where((slot == held) & (slot < end), 1.0, 0.0).astype(jnp.bfloat16)
    for giver in range(pair):
        for ext, outs in ((row_ext, (attn_out, dq_out)), (dk_ext, (dk_out,)), (dv_ext, (dv_out,))):
            placed = jnp.dot(pick, ext[giver], preferred_element_type=jnp.float32).astype(jnp.bfloat16)
            count = ext.shape[2] // len(outs)
            for index, out in enumerate(outs):
                out[:, pl.ds(giver * count, count)] = placed[:, index * count:(index + 1) * count]


def joint(sequence, groups, q_old, k_old, value_old_layout, dout_old, old_offsets, new_offsets):
    chunk = q_old.shape[0]
    pair = k_old.shape[1] // (groups * HEAD_SIZE)
    members = q_old.shape[1] // k_old.shape[1]
    levels = sequence // pair
    slots = chunk * groups
    slack = (slots - TOK_DEV) // 2
    rows = pair * TOK_DEV
    width = members * HEAD_SIZE
    lanes = members * rows
    bf16, f32 = jnp.bfloat16, jnp.float32
    vmem, dma = pltpu.VMEM, pltpu.SemaphoreType.DMA
    out = lambda count: jax.ShapeDtypeStruct((slots, count), bf16)
    smem = pl.BlockSpec(memory_space=pltpu.SMEM)
    anywhere = pl.BlockSpec(memory_space=pl.ANY)
    whole = pl.BlockSpec(memory_space=pltpu.VMEM)
    held = lambda count: jax.ShapeDtypeStruct((pair, slots, count), bf16)
    landed = pl.pallas_call(
        functools.partial(joint_kernel, levels, pair, groups, members),
        out_shape=(held(2 * width), held(HEAD_SIZE), held(HEAD_SIZE)),
        in_specs=[smem, anywhere, anywhere, anywhere, anywhere],
        out_specs=(whole,) * 3,
        scratch_shapes=[
            vmem((pair * groups, chunk, 2 * HEAD_SIZE), bf16),
            vmem((pair * groups, chunk, 2 * width), bf16),
            vmem((rows + 2 * slack, 2 * width), f32),
            vmem((rows + 2 * slack, 2 * HEAD_SIZE), bf16),
            vmem((rows + 2 * slack, 2 * width), bf16),
            vmem((2, slack, 2 * HEAD_SIZE), bf16),
            vmem((2, slack, 2 * width), bf16),
            vmem((levels, rows, HEAD_SIZE), bf16),
            vmem((levels, rows, HEAD_SIZE), bf16),
            vmem((lanes, HEAD_SIZE), bf16),
            vmem((lanes, HEAD_SIZE), bf16),
            vmem((levels, rows, lanes), f32),
            vmem((levels, rows, lanes), f32),
            vmem((2, levels, rows, HEAD_SIZE), bf16),
            vmem((2, levels, rows, HEAD_SIZE), bf16),
            vmem((2, rows, HEAD_SIZE), f32),
            vmem((HEAD_SIZE, lanes), f32),
            vmem((HEAD_SIZE, lanes), f32),
            vmem((rows, 2 * width), bf16),
            vmem((2, rows, HEAD_SIZE), bf16),
            dma((4, pair * groups)), dma((4, pair * groups)), dma((4,)),
            dma((2, 2)), dma((2, 2)),
            dma((2, levels)), dma((2, levels)),
            dma((2, levels)), dma((2, levels)),
            dma((3, pair + 2)), dma((3, pair, 3)), dma((3,)),
        ],
        compiler_params=pltpu.CompilerParams(
            collective_id=0, has_side_effects=True, vmem_limit_bytes=24 << 20),
    )(old_offsets, q_old, k_old, value_old_layout, dout_old)
    return pl.pallas_call(
        place_kernel,
        out_shape=(out(pair * width), out(pair * width), out(pair * HEAD_SIZE), out(pair * HEAD_SIZE)),
        in_specs=[smem] + [whole] * 3,
        out_specs=(whole,) * 4,
        compiler_params=pltpu.CompilerParams(vmem_limit_bytes=8 << 20),
    )(new_offsets, *landed)


def solution(mesh):
    sequence, groups = mesh.shape["seq"], mesh.shape["head"]
    covered = sequence * TOK_DEV <= ATTEND_WINDOW
    body = functools.partial(joint, sequence, groups) if covered else on_device
    return jax.shard_map(
        body,
        mesh=mesh,
        in_specs=(
            P(("seq", "head"), None),
            P(("seq", "head"), None),
            P(("seq", "head"), None),
            P(("seq", "head"), None),
            P(),
            P(),
        ),
        out_specs=(P("seq", "head"), P("seq", "head"), P("seq", "head"), P("seq", "head")),
        check_vma=False,
    )
```

```python
import functools

import jax
import jax.numpy as jnp
from jax import lax
from jax.experimental import pallas as pl
from jax.experimental.pallas import tpu as pltpu
from jax.sharding import PartitionSpec as P

TOK_DEV = 128
ATTEND_WINDOW = 1024
HEAD_SIZE = 128


query_scale = 168.0 ** (-0.5)


def shifted(value, axis, steps):
    count = lax.axis_size(axis)
    initial, last = (max(0, -steps), min(count, count - steps))
    return lax.ppermute(value, axis, [(source, source + steps) for source in range(initial, last)])


def relocate(row_data, source, target, slot_slack, out_rows):
    device = lax.axis_index("seq")
    own_rows = row_data.shape[0]
    first_row = source[device]
    end_row = source[device + 1]
    tail_start = jnp.maximum(end_row - first_row - slot_slack, 0)
    tail_rows = lax.dynamic_slice_in_dim(row_data, tail_start, slot_slack, 0)
    head_rows = row_data[:slot_slack]
    from_left = shifted(tail_rows, "seq", 1)
    from_right = shifted(head_rows, "seq", -1)
    before_row = source[jnp.maximum(device - 1, 0)]
    left_start = before_row + jnp.maximum(first_row - before_row - slot_slack, 0)
    candidates = jnp.concatenate([from_left, row_data, from_right], axis=0)
    targets = target[device] + jnp.arange(out_rows, dtype=jnp.int32)
    selected = jnp.where(
        targets < first_row,
        targets - left_start,
        jnp.where(
            targets < end_row,
            slot_slack + targets - first_row,
            slot_slack + own_rows + targets - end_row,
        ),
    )
    selected = jnp.clip(selected, 0, candidates.shape[0] - 1)
    is_live = targets < target[device + 1]
    return jnp.where(
        is_live[:, None], jnp.take(candidates, selected, axis=0), jnp.zeros((), row_data.dtype)
    )


def key_window(key_value, farthest, nearest):
    device = lax.axis_index("seq")
    devices = lax.axis_size("seq")
    gathered, places, live_parts = ([], [], [])
    for distance in range(farthest, nearest - 1, -1):
        if distance == 0:
            arrived = key_value
        else:
            arrived = shifted(key_value, "seq", distance)
        source_block = device - distance
        gathered.append(arrived)
        places.append(source_block * TOK_DEV + jnp.arange(TOK_DEV, dtype=jnp.int32))
        live_parts.append(jnp.full((TOK_DEV,), (source_block >= 0) & (source_block < devices)))
    return (jnp.concatenate(gathered, axis=0), jnp.concatenate(places), jnp.concatenate(live_parts))


def return_grads(grads, farthest, nearest):
    summed = None
    for position, distance in enumerate(range(farthest, nearest - 1, -1)):
        block = grads[position * TOK_DEV : (position + 1) * TOK_DEV]
        if distance == 0:
            arrived = block
        else:
            arrived = shifted(block, "seq", -distance)
        summed = arrived if summed is None else summed + arrived
    return summed


def attend(
    queries, grads_out, key_rows, value_rows, query_places, query_live, key_places, key_live
):
    head_count = queries.shape[1] // HEAD_SIZE
    kv_count = key_rows.shape[1] // HEAD_SIZE
    heads_per_group = head_count // kv_count
    gap_rows = query_places[:, None] - key_places[None, :]
    allowed = (gap_rows >= 0) & (gap_rows < ATTEND_WINDOW) & query_live[:, None] & key_live[None, :]
    contract_last = (((1,), (1,)), ((), ()))
    contract_first = (((0,), (0,)), ((), ()))
    attn_parts, query_grads, key_grads, value_grads = ([], [], [], [])
    for kv_head in range(kv_count):
        key_head = key_rows[:, kv_head * HEAD_SIZE : (kv_head + 1) * HEAD_SIZE]
        value_head = value_rows[:, kv_head * HEAD_SIZE : (kv_head + 1) * HEAD_SIZE]
        key_total = jnp.zeros((key_rows.shape[0], HEAD_SIZE), jnp.float32)
        value_total = jnp.zeros((key_rows.shape[0], HEAD_SIZE), jnp.float32)
        for member in range(heads_per_group):
            head_number = kv_head * heads_per_group + member
            query_head = queries[:, head_number * HEAD_SIZE : (head_number + 1) * HEAD_SIZE]
            grad_head = grads_out[:, head_number * HEAD_SIZE : (head_number + 1) * HEAD_SIZE]
            scores = (
                lax.dot_general(
                    query_head, key_head, contract_last, preferred_element_type=jnp.float32
                )
                * query_scale
            )
            scores = jnp.where(allowed, scores, -1e30)
            row_max = jnp.max(scores, axis=1, keepdims=True)
            weights = jnp.where(allowed, jnp.exp(scores - row_max), 0.0)
            row_total = jnp.sum(weights, axis=1, keepdims=True)
            probabilities = weights / jnp.where(query_live[:, None], row_total, 1.0)
            rounded = probabilities.astype(jnp.bfloat16)
            head_out = jnp.dot(rounded, value_head, preferred_element_type=jnp.float32).astype(
                jnp.bfloat16
            )
            row_delta = jnp.sum(
                grad_head.astype(jnp.float32) * head_out.astype(jnp.float32), axis=1, keepdims=True
            )
            grad_prob = lax.dot_general(
                grad_head, value_head, contract_last, preferred_element_type=jnp.float32
            )
            grad_score = (probabilities * (grad_prob - row_delta) * query_scale).astype(
                jnp.bfloat16
            )
            query_grads.append(
                jnp.dot(grad_score, key_head, preferred_element_type=jnp.float32).astype(
                    jnp.bfloat16
                )
            )
            key_total = key_total + lax.dot_general(
                grad_score, query_head, contract_first, preferred_element_type=jnp.float32
            )
            value_total = value_total + lax.dot_general(
                rounded, grad_head, contract_first, preferred_element_type=jnp.float32
            )
            attn_parts.append(head_out)
        key_grads.append(key_total)
        value_grads.append(value_total)
    return (
        jnp.concatenate(attn_parts, axis=1),
        jnp.concatenate(query_grads, axis=1),
        jnp.concatenate(key_grads, axis=1),
        jnp.concatenate(value_grads, axis=1),
    )


def on_device(q_old, k_old, value_old_layout, dout_old, old_offsets, new_offsets):
    query_rows, grad_rows, key_rows, value_rows = (
        lax.all_to_all(q_old, "head", split_axis=1, concat_axis=0, tiled=True),
        lax.all_to_all(dout_old, "head", split_axis=1, concat_axis=0, tiled=True),
        lax.all_to_all(k_old, "head", split_axis=1, concat_axis=0, tiled=True),
        lax.all_to_all(value_old_layout, "head", split_axis=1, concat_axis=0, tiled=True),
    )
    device = lax.axis_index("seq")
    devices = lax.axis_size("seq")
    even_offsets = jnp.arange(devices + 1, dtype=jnp.int32) * TOK_DEV
    query_width = query_rows.shape[1]
    key_width = key_rows.shape[1]
    slot_rows = query_rows.shape[0]
    slot_slack = (slot_rows - TOK_DEV) // 2
    halo_blocks = ATTEND_WINDOW // TOK_DEV
    relocated = relocate(
        jnp.concatenate([query_rows, grad_rows, key_rows, value_rows], axis=1),
        old_offsets,
        even_offsets,
        slot_slack,
        TOK_DEV,
    )
    queries = relocated[:, :query_width]
    grads_out = relocated[:, query_width : 2 * query_width]
    buffered, key_places, key_live = key_window(relocated[:, 2 * query_width :], halo_blocks, 0)
    query_places = device * TOK_DEV + jnp.arange(TOK_DEV, dtype=jnp.int32)
    query_live = jnp.full((TOK_DEV,), True)
    attn, grad_query, key_grad, value_grad = attend(
        queries,
        grads_out,
        buffered[:, :key_width],
        buffered[:, key_width:],
        query_places,
        query_live,
        key_places,
        key_live,
    )
    pair_grads = return_grads(
        jnp.concatenate([key_grad, value_grad], axis=1), halo_blocks, 0
    ).astype(jnp.bfloat16)
    placed = relocate(
        jnp.concatenate([attn, grad_query, pair_grads], axis=1),
        even_offsets,
        new_offsets,
        slot_slack,
        slot_rows,
    )
    attn_out = placed[:, :query_width]
    grad_query_out = placed[:, query_width : 2 * query_width]
    grad_key_out = placed[:, 2 * query_width : 2 * query_width + key_width]
    grad_value_out = placed[:, 2 * query_width + key_width :]
    return (attn_out, grad_query_out, grad_key_out, grad_value_out)


def joint_kernel(levels, pair, groups, members, *refs):
    (offsets_in, targets_in, q_in, k_in, v_in, d_in, row_ext, dk_ext, dv_ext, pick_out, old_offsets, new_offsets,
     kv_chunks, qd_chunks, wide, kv_wide, qd_wide, kv_halo, qd_halo, keys, values, queries, grads,
     probs, grad_probs, grad_send, grad_recv, grad_own, attn_t, dq_t, row_buf, grad_buf, in_send, in_recv, in_local, halo_send, halo_recv, cast_send, cast_recv, ret_send,
     ret_recv, out_send, out_recv, out_local, table_sem) = refs
    seq, column = lax.axis_index("seq"), lax.axis_index("head")
    level, part = seq // pair, seq % pair
    crowd = pair * groups
    me = part * groups + column
    chunk = k_in.shape[0]
    slots = chunk * groups
    slack = (slots - TOK_DEV) // 2
    rows = pair * TOK_DEV
    width = members * HEAD_SIZE
    f32, bf16 = jnp.float32, jnp.bfloat16

    def at(to_level, to_part, to_column):
        return {"seq": to_level * pair + to_part, "head": to_column}

    def send(src, dst, ssem, rsem, where):
        return pltpu.make_async_remote_copy(
            src_ref=src, dst_ref=dst, send_sem=ssem, recv_sem=rsem, device_id=where,
            device_id_type=pl.DeviceIdType.MESH)

    here = at(level, part, column)

    def landed(dst, rsem):
        send(dst, dst, rsem, rsem, here).wait_recv()

    def left(src, ssem):
        send(src, src, ssem, ssem, here).wait_send()

    tables = ((offsets_in, old_offsets), (targets_in, new_offsets))
    for index, (src, dst) in enumerate(tables):
        pltpu.make_async_copy(src, dst, table_sem.at[index]).start()
    barrier = pltpu.get_barrier_semaphore()
    for step in range(1, crowd):
        peer = lax.rem(me + step, crowd)
        pl.semaphore_signal(barrier, inc=1, device_id=at(level, peer // groups, peer % groups),
                            device_id_type=pl.DeviceIdType.MESH)
    for step in range(1, levels):
        for other in range(pair):
            pl.semaphore_signal(barrier, inc=1, device_id=at(lax.rem(level + step, levels), other, column),
                                device_id_type=pl.DeviceIdType.MESH)
    pl.semaphore_wait(barrier, crowd - 1 + (levels - 1) * pair)

    def pieces(owner, source):
        head = (owner % groups) * pair + owner // groups
        k_at = pl.ds(pl.multiple_of(head * HEAD_SIZE, HEAD_SIZE), HEAD_SIZE)
        q_at = pl.ds(pl.multiple_of(head * width, HEAD_SIZE), width)
        return (
            (k_in.at[:, k_at], kv_chunks.at[source, :, pl.ds(0, HEAD_SIZE)]),
            (v_in.at[:, k_at], kv_chunks.at[source, :, pl.ds(HEAD_SIZE, HEAD_SIZE)]),
            (q_in.at[:, q_at], qd_chunks.at[source, :, pl.ds(0, width)]),
            (d_in.at[:, q_at], qd_chunks.at[source, :, pl.ds(width, width)]),
        )

    for kinds in ((0, 1), (2, 3)):
        for step in range(crowd):
            peer = lax.rem(me + step, crowd)
            for kind in kinds:
                src, dst = pieces(peer, me)[kind]
                if step == 0:
                    pltpu.make_async_copy(src, dst, in_local.at[kind]).start()
                else:
                    send(src, dst, in_send.at[kind, step], in_recv.at[kind, step],
                         at(level, peer // groups, peer % groups)).start()

    def arrive(kinds):
        for kind in kinds:
            src, dst = pieces(me, me)[kind]
            pltpu.make_async_copy(src, dst, in_local.at[kind]).wait()
            for step in range(1, crowd):
                source = lax.rem(me + crowd - step, crowd)
                landed(pieces(me, source)[kind][1], in_recv.at[kind, step])

    def spread(chunks, target):
        count = chunks.shape[2]
        wide[:, pl.ds(0, count)] = jnp.zeros((rows + 2 * slack, count), f32)
        row = lax.broadcasted_iota(jnp.int32, (slots, chunk), 0)
        slot = lax.broadcasted_iota(jnp.int32, (slots, chunk), 1)
        for other in range(pair):
            block = level * pair + other
            first, end = old_offsets[block], old_offsets[block + 1]
            total = jnp.zeros((slots, count), f32)
            for piece in range(groups):
                place = slot + (first + piece * chunk)
                pick = (row + (block * TOK_DEV - slack) == place) & (place < end)
                total = total + jnp.dot(jnp.where(pick, 1.0, 0.0).astype(bf16),
                                        chunks[other * groups + piece], preferred_element_type=f32)
            span = pl.ds(other * TOK_DEV, slots)
            wide[span, pl.ds(0, count)] = wide[span, pl.ds(0, count)] + total
        target[...] = wide[:, pl.ds(0, count)].astype(bf16)

    def halo(kind, source, dest):
        down = (source.at[pl.ds(0, slack)], dest.at[1])
        up = (source.at[pl.ds(rows + slack, slack)], dest.at[0])

        @pl.when(level > 0)
        def _():
            send(*down, halo_send.at[kind, 1], halo_recv.at[kind, 1], at(level - 1, part, column)).start()

        @pl.when(level < levels - 1)
        def _():
            send(*up, halo_send.at[kind, 0], halo_recv.at[kind, 0], at(level + 1, part, column)).start()

        def finish():
            @pl.when(level > 0)
            def _():
                landed(dest.at[0], halo_recv.at[kind, 0])

            @pl.when(level == 0)
            def _():
                dest[0] = jnp.zeros(dest.shape[1:], bf16)

            @pl.when(level < levels - 1)
            def _():
                landed(dest.at[1], halo_recv.at[kind, 1])

            @pl.when(level == levels - 1)
            def _():
                dest[1] = jnp.zeros(dest.shape[1:], bf16)

            return jnp.concatenate([
                source[pl.ds(slack, slack)] + dest[0],
                source[pl.ds(2 * slack, rows - 2 * slack)],
                source[pl.ds(rows, slack)] + dest[1],
            ], axis=0)

        return finish

    for index, (src, dst) in enumerate(tables):
        pltpu.make_async_copy(src, dst, table_sem.at[index]).wait()
    first, end = new_offsets[seq], new_offsets[seq + 1]
    slot = lax.broadcasted_iota(jnp.int32, (slots, slots), 0) + first
    held = lax.broadcasted_iota(jnp.int32, (slots, slots), 1) + (seq * TOK_DEV - slack)
    pick_out[...] = jnp.where((slot == held) & (slot < end), 1.0, 0.0).astype(bf16)
    arrive((0, 1))
    spread(kv_chunks, kv_wide)
    block = halo(0, kv_wide, kv_halo)()
    keys[level] = block[:, :HEAD_SIZE]
    values[level] = block[:, HEAD_SIZE:]

    def forward(step):
        @pl.when(level < levels - 1)
        def _():
            send(keys.at[level - step], keys.at[level - step], cast_send.at[0, step],
                 cast_recv.at[0, step + 1], at(level + 1, part, column)).start()

    forward(0)
    if levels > 1:
        @pl.when(level > 0)
        def _():
            landed(keys.at[level - 1], cast_recv.at[0, 1])
            forward(1)

    arrive((2, 3))
    spread(qd_chunks, qd_wide)
    finish = halo(1, qd_wide, qd_halo)
    for step in range(1, levels):
        @pl.when(level + step < levels)
        def _():
            send(values.at[level], values.at[level], cast_send.at[1, step],
                 cast_recv.at[1, step], at(level + step, part, column)).start()
    block = finish()
    for member in range(members):
        span = pl.ds(member * rows, rows)
        queries[span] = block[:, member * HEAD_SIZE:(member + 1) * HEAD_SIZE]
        grads[span] = block[:, width + member * HEAD_SIZE:width + (member + 1) * HEAD_SIZE]

    nt = (((1,), (1,)), ((), ()))
    tn = (((0,), (0,)), ((), ()))
    lanes = members * rows

    def score_step(step, row_max):
        @pl.when(step > 1)
        def _():
            landed(keys.at[level - step], cast_recv.at[0, step])
            forward(step)

        score = lax.dot_general(keys[level - step], queries[...], nt, preferred_element_type=f32) * query_scale
        key_place = lax.broadcasted_iota(jnp.int32, (rows, rows), 0)
        query_place = lax.broadcasted_iota(jnp.int32, (rows, rows), 1) + step * rows
        allowed = jnp.concatenate([key_place <= query_place] * members, axis=1)
        score = jnp.where(allowed, score, -1e30)
        probs[level - step] = score
        return jnp.maximum(row_max, jnp.max(score, axis=0, keepdims=True))

    row_max = lax.fori_loop(0, level + 1, score_step, jnp.full((1, lanes), -1e30, f32))

    def weight_step(step, total):
        weight = jnp.exp(probs[step] - row_max)
        probs[step] = weight
        return total + jnp.sum(weight, axis=0, keepdims=True)

    row_total = lax.fori_loop(0, level + 1, weight_step, jnp.zeros((1, lanes), f32))
    inverse = 1.0 / row_total

    def share(kind, low, term):
        @pl.when(low < level)
        def _():
            grad_send[kind, low] = term.astype(bf16)
            send(grad_send.at[kind, low], grad_recv.at[kind, level - low], ret_send.at[kind, level - low],
                 ret_recv.at[kind, level - low], at(low, part, column)).start()

        @pl.when(low == level)
        def _():
            grad_own[kind] = term

    def prob_step(low, carry):
        prob = probs[low] * inverse
        probs[low] = prob
        share(0, low, jnp.dot(prob.astype(bf16), grads[...], preferred_element_type=f32))
        return carry

    lax.fori_loop(0, level + 1, prob_step, 0)
    attn_t[...] = jnp.zeros_like(attn_t)

    def value_step(step, carry):
        @pl.when(step > 0)
        def _():
            landed(values.at[level - step], cast_recv.at[1, step])

        prob = probs[level - step].astype(bf16)
        attn_t[...] += lax.dot_general(values[level - step], prob, tn, preferred_element_type=f32)
        grad_probs[level - step] = lax.dot_general(values[level - step], grads[...], nt, preferred_element_type=f32)
        return carry

    lax.fori_loop(0, level + 1, value_step, 0)
    attn = attn_t[...].astype(bf16).astype(f32)
    delta = jnp.sum(attn * jnp.transpose(grads[...].astype(f32)), axis=0, keepdims=True)
    attn = jnp.transpose(attn).astype(bf16)
    dq_t[...] = jnp.zeros_like(dq_t)

    def grad_step(low, carry):
        prob = probs[low]
        change = (prob * (grad_probs[low] - delta) * query_scale).astype(bf16)
        dq_t[...] += lax.dot_general(keys[low], change, tn, preferred_element_type=f32)
        share(1, low, jnp.dot(change, queries[...], preferred_element_type=f32))
        return carry

    lax.fori_loop(0, level + 1, grad_step, 0)
    dq = jnp.transpose(dq_t[...]).astype(bf16)
    for member in range(members):
        span = slice(member * rows, (member + 1) * rows)
        row_buf[:, pl.ds(member * HEAD_SIZE, HEAD_SIZE)] = attn[span]
        row_buf[:, pl.ds(width + member * HEAD_SIZE, HEAD_SIZE)] = dq[span]

    def routes(other):
        begin = other * TOK_DEV - slack
        low, high = max(0, begin), min(rows, begin + slots)
        return pl.ds(low, high - low), pl.ds(low - begin, high - low)

    head_span, tail_span = pl.ds(0, slack), pl.ds(slots - slack, slack)
    last_span = pl.ds(rows - slack, slack)

    def hand_out(kind, source, dest):
        for other in range(pair):
            take, put = routes(other)

            @pl.when(part == other)
            def _():
                pltpu.make_async_copy(source.at[take], dest.at[part, put], out_local.at[kind]).start()

            @pl.when(part != other)
            def _():
                send(source.at[take], dest.at[part, put], out_send.at[kind, other],
                     out_recv.at[kind, part, 0], at(level, other, column)).start()

        @pl.when(level < levels - 1)
        def _():
            send(source.at[last_span], dest.at[part, head_span], out_send.at[kind, pair],
                 out_recv.at[kind, part, 1], at(level + 1, 0, column)).start()

        @pl.when(level > 0)
        def _():
            send(source.at[head_span], dest.at[part, tail_span], out_send.at[kind, pair + 1],
                 out_recv.at[kind, part, 2], at(level - 1, pair - 1, column)).start()

    def take_in(kind, source, dest):
        for other in range(pair):
            take, put = routes(other)

            @pl.when(part == other)
            def _():
                pltpu.make_async_copy(source.at[take], dest.at[part, put], out_local.at[kind]).wait()
                for giver in range(pair):
                    if giver != other:
                        landed(dest.at[giver, put], out_recv.at[kind, giver, 0])

            @pl.when(part != other)
            def _():
                left(source.at[take], out_send.at[kind, other])

        for giver in range(pair):
            @pl.when((part == 0) & (level > 0))
            def _():
                landed(dest.at[giver, head_span], out_recv.at[kind, giver, 1])

            @pl.when((part == 0) & (level == 0))
            def _():
                dest[giver, head_span] = jnp.zeros((slack, dest.shape[2]), bf16)

            @pl.when((part == pair - 1) & (level < levels - 1))
            def _():
                landed(dest.at[giver, tail_span], out_recv.at[kind, giver, 2])

            @pl.when((part == pair - 1) & (level == levels - 1))
            def _():
                dest[giver, tail_span] = jnp.zeros((slack, dest.shape[2]), bf16)

        @pl.when(level < levels - 1)
        def _():
            left(source.at[last_span], out_send.at[kind, pair])

        @pl.when(level > 0)
        def _():
            left(source.at[head_span], out_send.at[kind, pair + 1])

    hand_out(0, row_buf, row_ext)
    for kind, dest in ((0, dv_ext), (1, dk_ext)):
        for step in range(1, levels):
            @pl.when(level + step < levels)
            def _():
                landed(grad_recv.at[kind, step], ret_recv.at[kind, step])
                grad_own[kind] += grad_recv[kind, step].astype(f32)
        grad_buf[kind] = grad_own[kind].astype(bf16)
        hand_out(1 + kind, grad_buf.at[kind], dest)
    take_in(0, row_buf, row_ext)
    take_in(1, grad_buf.at[0], dv_ext)
    take_in(2, grad_buf.at[1], dk_ext)

    for kind in range(4):
        for step in range(1, crowd):
            left(pieces(me, me)[kind][0], in_send.at[kind, step])
    for kind, source in ((0, kv_wide), (1, qd_wide)):
        @pl.when(level > 0)
        def _():
            left(source.at[pl.ds(0, slack)], halo_send.at[kind, 1])

        @pl.when(level < levels - 1)
        def _():
            left(source.at[pl.ds(rows + slack, slack)], halo_send.at[kind, 0])
    for step in range(1, levels):
        @pl.when(level + step < levels)
        def _():
            left(values.at[level], cast_send.at[1, step])

        @pl.when((level < levels - 1) & (level >= step - 1))
        def _():
            left(keys.at[level - step + 1], cast_send.at[0, step - 1])

        @pl.when(level >= step)
        def _():
            for kind in range(2):
                left(grad_send.at[kind, level - step], ret_send.at[kind, step])


def place_kernel(row_ext, dk_ext, dv_ext, pick, attn_out, dq_out, dk_out, dv_out):
    pair = row_ext.shape[0]
    for giver in range(pair):
        for ext, outs in ((row_ext, (attn_out, dq_out)), (dk_ext, (dk_out,)), (dv_ext, (dv_out,))):
            placed = jnp.dot(pick[...], ext[giver], preferred_element_type=jnp.float32).astype(jnp.bfloat16)
            count = ext.shape[2] // len(outs)
            for index, out in enumerate(outs):
                out[:, pl.ds(giver * count, count)] = placed[:, index * count:(index + 1) * count]


def joint(sequence, groups, q_old, k_old, value_old_layout, dout_old, old_offsets, new_offsets):
    chunk = q_old.shape[0]
    pair = k_old.shape[1] // (groups * HEAD_SIZE)
    members = q_old.shape[1] // k_old.shape[1]
    levels = sequence // pair
    slots = chunk * groups
    slack = (slots - TOK_DEV) // 2
    rows = pair * TOK_DEV
    width = members * HEAD_SIZE
    lanes = members * rows
    bf16, f32 = jnp.bfloat16, jnp.float32
    vmem, dma = pltpu.VMEM, pltpu.SemaphoreType.DMA
    out = lambda count: jax.ShapeDtypeStruct((slots, count), bf16)
    anywhere = pl.BlockSpec(memory_space=pltpu.HBM)
    whole = pl.BlockSpec(memory_space=pltpu.VMEM)
    held = lambda count: jax.ShapeDtypeStruct((pair, slots, count), bf16)
    landed = pl.pallas_call(
        functools.partial(joint_kernel, levels, pair, groups, members),
        out_shape=(held(2 * width), held(HEAD_SIZE), held(HEAD_SIZE), out(slots)),
        in_specs=[anywhere] * 6,
        out_specs=(whole,) * 4,
        scratch_shapes=[
            pltpu.SMEM(old_offsets.shape, jnp.int32),
            pltpu.SMEM(new_offsets.shape, jnp.int32),
            vmem((pair * groups, chunk, 2 * HEAD_SIZE), bf16),
            vmem((pair * groups, chunk, 2 * width), bf16),
            vmem((rows + 2 * slack, 2 * width), f32),
            vmem((rows + 2 * slack, 2 * HEAD_SIZE), bf16),
            vmem((rows + 2 * slack, 2 * width), bf16),
            vmem((2, slack, 2 * HEAD_SIZE), bf16),
            vmem((2, slack, 2 * width), bf16),
            vmem((levels, rows, HEAD_SIZE), bf16),
            vmem((levels, rows, HEAD_SIZE), bf16),
            vmem((lanes, HEAD_SIZE), bf16),
            vmem((lanes, HEAD_SIZE), bf16),
            vmem((levels, rows, lanes), f32),
            vmem((levels, rows, lanes), f32),
            vmem((2, levels, rows, HEAD_SIZE), bf16),
            vmem((2, levels, rows, HEAD_SIZE), bf16),
            vmem((2, rows, HEAD_SIZE), f32),
            vmem((HEAD_SIZE, lanes), f32),
            vmem((HEAD_SIZE, lanes), f32),
            vmem((rows, 2 * width), bf16),
            vmem((2, rows, HEAD_SIZE), bf16),
            dma((4, pair * groups)), dma((4, pair * groups)), dma((4,)),
            dma((2, 2)), dma((2, 2)),
            dma((2, levels)), dma((2, levels)),
            dma((2, levels)), dma((2, levels)),
            dma((3, pair + 2)), dma((3, pair, 3)), dma((3,)), dma((2,)),
        ],
        compiler_params=pltpu.CompilerParams(
            collective_id=0, has_side_effects=True, vmem_limit_bytes=66400000),
    )(old_offsets, new_offsets, q_old, k_old, value_old_layout, dout_old)
    return pl.pallas_call(
        place_kernel,
        out_shape=(out(pair * width), out(pair * width), out(pair * HEAD_SIZE), out(pair * HEAD_SIZE)),
        in_specs=[whole] * 4,
        out_specs=(whole,) * 4,
        compiler_params=pltpu.CompilerParams(vmem_limit_bytes=66400000),
    )(*landed)


def solution(mesh):
    sequence, groups = mesh.shape["seq"], mesh.shape["head"]
    covered = sequence * TOK_DEV <= ATTEND_WINDOW
    body = functools.partial(joint, sequence, groups) if covered else on_device
    return jax.shard_map(
        body,
        mesh=mesh,
        in_specs=(
            P(("seq", "head"), None),
            P(("seq", "head"), None),
            P(("seq", "head"), None),
            P(("seq", "head"), None),
            P(),
            P(),
        ),
        out_specs=(P("seq", "head"), P("seq", "head"), P("seq", "head"), P("seq", "head")),
        check_vma=False,
    )
```
